32 devices in a mesh: dp: 8 (over z, y), tensor: 4 (over x, core).
Axes of the slice: x: 2, y: 2, z: 4, core: 2. Of those that a mesh axis runs over, the one named last changes fastest.
Arguments:
- layer_input: bfloat16 [8192, 2048], P(('dp', 'tensor')), may hold values from -6 to 6
- out_grad: bfloat16 [8192, 2048], P(('dp', 'tensor')), may hold values from -6 to 6
- prefix_length: int32 [8], P('dp'), may hold values from 102 to 512, as said below
- positions: int32 [8192], P('dp'), may hold values from 0 to 4094, as said below
- attn_gain: float32 [2048], replicated, may hold values from 0.5 to 1.5
- w_query: bfloat16 [2048, 2048], P('dp', 'tensor'), may hold values from -0.125 to 0.125
- key_projection: bfloat16 [2048, 1024], P('dp', 'tensor'), may hold values from -0.125 to 0.125
- value_projection: bfloat16 [2048, 1024], P('dp', 'tensor'), may hold values from -0.125 to 0.125
- query_gain: float32 [128], replicated, may hold values from 0.5 to 1.5
- key_norm_gain: float32 [128], replicated, may hold values from 0.5 to 1.5
- w_out: bfloat16 [2048, 2048], P('tensor', 'dp'), may hold values from -3 to 3
- mlp_gain: float32 [2048], replicated, may hold values from 0.5 to 1.5
- w_gate: bfloat16 [2048, 6144], P('dp', 'tensor'), may hold values from -0.125 to 0.125
- w_up: bfloat16 [2048, 6144], P('dp', 'tensor'), may hold values from -0.125 to 0.125
- w_down: bfloat16 [6144, 2048], P('tensor', 'dp'), may hold values from -0.078125 to 0.078125
Outputs:
- layer_output: bfloat16 [8192, 2048], P(('dp', 'tensor'))
- input_grad: bfloat16 [8192, 2048], P(('dp', 'tensor'))
- attn_gain_grad: float32 [2048], replicated
- w_query_grad: float32 [2048, 2048], P('dp', 'tensor')
- w_key_grad: float32 [2048, 1024], P('dp', 'tensor')
- w_value_grad: float32 [2048, 1024], P('dp', 'tensor')
- query_gain_grad: float32 [128], replicated
- key_gain_grad: float32 [128], replicated
- w_out_grad: float32 [2048, 2048], P('tensor', 'dp')
- mlp_gain_grad: float32 [2048], replicated
- w_gate_grad: float32 [2048, 6144], P('dp', 'tensor')
- w_up_grad: float32 [2048, 6144], P('dp', 'tensor')
- w_down_grad: float32 [6144, 2048], P('tensor', 'dp')
The draws below stay inside these ranges and needn't reach their ends.
Inputs may be any that keep to these rules, and one draw needn't show every extreme that they name: `prefix_length`: the keys of a sequence before its prefix length are visible to all of its queries. Within a sequence the positions rise by one or two from one token to the next.
All inputs are finite; a program needn't handle non-finite values.
Results may differ from the reference program's by a relative error of at most 0.018.
Values may be sent and summed in bfloat16 or wider, within the bound.
No kernel may reach another device: no remote copies, remote signals or barrier semaphores. Data moves between devices by JAX's collectives and lax.ppermute only.
A program may use at most 192 MiB of HBM per device.

```python
import jax
import jax.numpy as jnp
from jax import lax

MODEL_WIDTH = 2048
QUERY_HEADS = 16
KEY_VALUE_HEADS = 8
HEAD_SIZE = 128
FF = 6144
SEQUENCE_LENGTH = 1024
SEQUENCE_COUNT = 8
TOKENS = 8192


def pick_two(key, count):
    first = jax.random.randint(jax.random.fold_in(key, 11), (), 0, count)
    step = jax.random.randint(jax.random.fold_in(key, 12), (), 1, count)
    return (first, (first + step) % count)


def draw_prefix_length(key, part):
    lengths = jax.random.randint(jax.random.fold_in(key, 1), (SEQUENCE_COUNT,), SEQUENCE_LENGTH // 10, SEQUENCE_LENGTH // 2 + 1)
    first, second = pick_two(jax.random.fold_in(key, 2), SEQUENCE_COUNT)
    lengths = lengths.at[first].set(SEQUENCE_LENGTH // 2).at[second].set(SEQUENCE_LENGTH // 10)
    return lengths.astype(jnp.int32)


def draw_positions(key, part):
    starts = jax.random.randint(jax.random.fold_in(key, 3), (SEQUENCE_COUNT,), 0, 2049)
    strides = jax.random.randint(jax.random.fold_in(key, 5), (SEQUENCE_COUNT, SEQUENCE_LENGTH), 1, 3)
    first, second = pick_two(jax.random.fold_in(key, 4), SEQUENCE_COUNT)
    starts = starts.at[first].set(2048).at[second].set(0)
    strides = strides.at[first].set(2)
    strides = strides.at[:, 0].set(0)
    offsets = jnp.cumsum(strides, axis=1)
    return (starts[:, None] + offsets).reshape(SEQUENCE_COUNT * SEQUENCE_LENGTH).astype(jnp.int32)


def shard_levels(own_key, dims, pieces, least, high):
    level = 1.0
    for axis_at, shards_of in pieces:
        steps = jax.random.uniform(jax.random.fold_in(jax.random.fold_in(own_key, 6), axis_at), (shards_of,), jnp.float32, least / len(pieces), high / len(pieces))
        level = level * jnp.repeat(jnp.exp(steps), dims[axis_at] // shards_of).reshape((-1,) + (1,) * (len(dims) - 1 - axis_at))
    return level


def centred(key, shape, deviation, most, pieces=(), kind=jnp.bfloat16):
    entries = jax.random.normal(key, shape, jnp.float32) * deviation
    if len(pieces) > 0:
        entries = shard_levels(key, shape, pieces, -0.22, 0.18) * entries
    return jnp.clip(entries, min=-most, max=most).astype(kind)


def setup_inputs(seed: int = 0) -> dict:
    arg_keys = jax.random.split(jax.random.key(seed), 16)
    layer_input = centred(arg_keys[0], (TOKENS, MODEL_WIDTH), 1.0, 6.0, ((0, 32),))
    out_grad = centred(arg_keys[1], (TOKENS, MODEL_WIDTH), 1.0, 6.0, ((0, 32),))
    prefix_length = draw_prefix_length(jax.random.fold_in(arg_keys[15], 71), 0)
    positions = draw_positions(jax.random.fold_in(arg_keys[15], 71), 0)
    attn_gain = jnp.clip(1.0 + 0.1 * jax.random.normal(arg_keys[4], (MODEL_WIDTH,), jnp.float32), 0.5, 1.5)
    w_query = centred(arg_keys[5], (MODEL_WIDTH, QUERY_HEADS * HEAD_SIZE), MODEL_WIDTH ** -0.5, 0.125, ((0, 8), (1, 4)))
    key_projection = centred(arg_keys[6], (MODEL_WIDTH, KEY_VALUE_HEADS * HEAD_SIZE), MODEL_WIDTH ** -0.5, 0.125, ((0, 8), (1, 4)))
    value_projection = centred(arg_keys[7], (MODEL_WIDTH, KEY_VALUE_HEADS * HEAD_SIZE), MODEL_WIDTH ** -0.5, 0.125, ((0, 8), (1, 4)))
    query_gain = jnp.clip(1.0 + 0.1 * jax.random.normal(arg_keys[8], (HEAD_SIZE,), jnp.float32), 0.5, 1.5)
    key_norm_gain = jnp.clip(1.0 + 0.1 * jax.random.normal(arg_keys[9], (HEAD_SIZE,), jnp.float32), 0.5, 1.5)
    w_out = centred(arg_keys[10], (QUERY_HEADS * HEAD_SIZE, MODEL_WIDTH), (max(1, 2 * QUERY_HEADS * HEAD_SIZE // SEQUENCE_LENGTH)) ** -0.5, 3.0, ((0, 4), (1, 8)))
    mlp_gain = jnp.clip(1.0 + 0.1 * jax.random.normal(arg_keys[11], (MODEL_WIDTH,), jnp.float32), 0.5, 1.5)
    w_gate = centred(arg_keys[12], (MODEL_WIDTH, FF), MODEL_WIDTH ** -0.5, 0.125, ((0, 8), (1, 4)))
    w_up = centred(arg_keys[13], (MODEL_WIDTH, FF), MODEL_WIDTH ** -0.5, 0.125, ((0, 8), (1, 4)))
    w_down = centred(arg_keys[14], (FF, MODEL_WIDTH), FF ** -0.5, 0.078125, ((0, 4), (1, 8)))
    return dict(layer_input=layer_input, out_grad=out_grad, prefix_length=prefix_length, positions=positions, attn_gain=attn_gain, w_query=w_query, key_projection=key_projection, value_projection=value_projection, query_gain=query_gain, key_norm_gain=key_norm_gain, w_out=w_out, mlp_gain=mlp_gain, w_gate=w_gate, w_up=w_up, w_down=w_down)


EPS = 1e-06
THETA = 1000000.0
HIGH = lax.Precision.HIGHEST

@jax.custom_vjp
def low(v):
    return lax.optimization_barrier(v.astype(jnp.bfloat16)).astype(jnp.float32)

@jax.custom_vjp
def low_back(v):
    return v

def low_keep(v):
    return (low(v), None)

def low_pass(kept, grad):
    return (grad,)

def back_keep(v):
    return (v, None)

def back_low(kept, grad):
    return (low(grad),)
low.defvjp(low_keep, low_pass)
low_back.defvjp(back_keep, back_low)

def root_mean_scale(value_heads, gain):
    return value_heads * lax.rsqrt(lax.optimization_barrier(jnp.mean(value_heads * value_heads, axis=-1, keepdims=True)) + EPS) * gain

def apply_rotary(value_heads, cosine_table, sine_table):
    half = value_heads.shape[-1] // 2
    first = value_heads[..., :half]
    second = value_heads[..., half:]
    return jnp.concatenate([first * cosine_table - second * sine_table, second * cosine_table + first * sine_table], axis=-1)

def matmul(left, right):
    return jnp.dot(left, right, precision=HIGH, preferred_element_type=jnp.float32)

def attend(query_heads, key_heads, value_heads, prefix):
    length = query_heads.shape[0]
    scores = low_back(jnp.einsum('qkgd,skd->kgqs', query_heads, key_heads, precision=HIGH) * HEAD_SIZE ** (-0.5))
    row_place = lax.broadcasted_iota(jnp.int32, (length, length), 0)
    col_place = lax.broadcasted_iota(jnp.int32, (length, length), 1)
    visible = (col_place <= row_place) | (col_place < prefix)
    scores = jnp.where(visible, scores, -jnp.inf)
    largest = lax.optimization_barrier(jnp.max(scores, axis=-1, keepdims=True))
    weights = jnp.exp(scores - largest)
    probs = low(weights / lax.optimization_barrier(jnp.sum(weights, axis=-1, keepdims=True)))
    return jnp.einsum('kgqs,skd->qkgd', probs, value_heads, precision=HIGH)

def attend_one(sequence_parts):
    return jax.checkpoint(attend)(sequence_parts[0], sequence_parts[1], sequence_parts[2], sequence_parts[3])

def layer(inputs, params, prefix_length, positions):
    attn_gain, w_query, key_projection, value_projection, query_gain, key_norm_gain, w_out, mlp_gain, w_gate, w_up, w_down = params
    token_count = inputs.shape[0]
    query_groups = QUERY_HEADS // KEY_VALUE_HEADS
    normed = low(root_mean_scale(inputs, attn_gain))
    query = low_back(matmul(normed, w_query))
    key = low_back(matmul(normed, key_projection))
    value_heads = low_back(low(matmul(normed, value_projection)))
    half = HEAD_SIZE // 2
    frequency = jnp.power(THETA, -(2.0 * jnp.arange(half, dtype=jnp.float32)) / HEAD_SIZE)
    angle = positions.astype(jnp.float32)[:, None] * frequency[None, :]
    cosine_table = jnp.cos(angle)[:, None, :]
    sine_table = jnp.sin(angle)[:, None, :]
    query_heads = low(apply_rotary(root_mean_scale(query.reshape(token_count, QUERY_HEADS, HEAD_SIZE), query_gain), cosine_table, sine_table))
    key_heads = low(apply_rotary(root_mean_scale(key.reshape(token_count, KEY_VALUE_HEADS, HEAD_SIZE), key_norm_gain), cosine_table, sine_table))
    sequence_parts = (query_heads.reshape(SEQUENCE_COUNT, SEQUENCE_LENGTH, KEY_VALUE_HEADS, query_groups, HEAD_SIZE), key_heads.reshape(SEQUENCE_COUNT, SEQUENCE_LENGTH, KEY_VALUE_HEADS, HEAD_SIZE), value_heads.reshape(SEQUENCE_COUNT, SEQUENCE_LENGTH, KEY_VALUE_HEADS, HEAD_SIZE), prefix_length)
    mixed = lax.map(attend_one, sequence_parts)
    mixed = low_back(low(mixed.reshape(token_count, QUERY_HEADS * HEAD_SIZE)))
    hidden = inputs + low_back(matmul(mixed, w_out))
    normed_second = low(root_mean_scale(hidden, mlp_gain))
    gate = low_back(matmul(normed_second, w_gate))
    upward = low_back(matmul(normed_second, w_up))
    activated = low(jax.nn.silu(gate) * upward)
    return hidden + low_back(matmul(activated, w_down))

def reference(layer_input, out_grad, prefix_length, positions, attn_gain, w_query, key_projection, value_projection, query_gain, key_norm_gain, w_out, mlp_gain, w_gate, w_up, w_down):
    params = tuple((p.astype(jnp.float32) for p in (attn_gain, w_query, key_projection, value_projection, query_gain, key_norm_gain, w_out, mlp_gain, w_gate, w_up, w_down)))

    def forward(inputs, weights):
        return layer(inputs, weights, prefix_length, positions)
    output, pull = jax.vjp(forward, layer_input.astype(jnp.float32), params)
    input_grad, grads = pull(out_grad.astype(jnp.float32))
    return (output.astype(jnp.bfloat16), input_grad.astype(jnp.bfloat16), grads[0], grads[1], grads[2], grads[3], grads[4], grads[5], grads[6], grads[7], grads[8], grads[9], grads[10])
```

```python
import jax
import jax.numpy as jnp
from jax import lax
from jax.sharding import PartitionSpec as P

HEAD_SIZE = 128
SEQUENCE_LENGTH = 1024
EPS = 1e-06
THETA = 1000000.0
PAIR = 2


def inverse_rms(value_heads):
    return lax.rsqrt(jnp.mean(value_heads * value_heads, axis=-1, keepdims=True) + EPS)


def norm_back(grad, unit, inverse, gain):
    scaled = grad * gain
    return inverse * (scaled - unit * jnp.mean(scaled * unit, axis=-1, keepdims=True))


def apply_rotary(value_heads, cosine_table, sine_table):
    half = value_heads.shape[-1] // 2
    first = value_heads[..., :half]
    second = value_heads[..., half:]
    return jnp.concatenate(
        [first * cosine_table - second * sine_table, second * cosine_table + first * sine_table],
        axis=-1,
    )


def dot(equation, left, right):
    return jnp.einsum(equation, left, right, preferred_element_type=jnp.float32)


def low(value):
    return value.astype(jnp.bfloat16)


def wide(value):
    return value.astype(jnp.float32)


def build(dp_size, tensor_size):
    ring = dp_size // PAIR
    ring_perm = [
        (a * PAIR + b, ((a + 1) % ring) * PAIR + b) for a in range(ring) for b in range(PAIR)
    ]
    pair_perm = [(i, i ^ 1) for i in range(dp_size)]
    across_perm = [(i, i ^ 2) for i in range(tensor_size)]
    core_perm = [(i, i ^ 1) for i in range(tensor_size)]

    def ring_shift(value):
        return lax.ppermute(value, "dp", ring_perm)

    def pair_swap(value):
        return lax.ppermute(value, "dp", pair_perm)

    def across_swap(value):
        return lax.ppermute(value, "tensor", across_perm)

    def core_swap(value):
        return lax.ppermute(value, "tensor", core_perm)

    def gather_weight(shard, axis):
        pieces = []
        held = shard
        for step in range(ring):
            pieces.append(held)
            pieces.append(pair_swap(held))
            if step < ring - 1:
                held = ring_shift(held)
        return jnp.concatenate(pieces, axis=axis)

    def scatter_grad(chunk):
        total = None
        for step in range(1, ring + 1):
            place = step % ring
            arrived = pair_swap(low(chunk(PAIR * place + 1)))
            part = chunk(PAIR * place) + wide(arrived)
            if total is not None:
                part = part + wide(ring_shift(low(total)))
            total = part
        return total

    def gather_rows(rows):
        far = across_swap(rows)
        return jnp.concatenate([rows, core_swap(rows), far, core_swap(far)], axis=0)

    def scatter_rows(parts):
        near = core_swap(low(parts(3)))
        send = low(parts(2) + wide(near))
        far = across_swap(send)
        close = core_swap(low(parts(1)))
        return parts(0) + wide(close) + wide(far)

    def local(
        layer_input,
        out_grad,
        prefix_length,
        positions,
        attn_gain,
        w_query,
        key_projection,
        value_projection,
        query_gain,
        key_norm_gain,
        w_out,
        mlp_gain,
        w_gate,
        w_up,
        w_down,
    ):
        head_q = w_query.shape[1] // HEAD_SIZE
        head_kv = key_projection.shape[1] // HEAD_SIZE
        query_groups = head_q // head_kv
        width_q = head_q * HEAD_SIZE
        width_kv = head_kv * HEAD_SIZE
        hidden_units = w_gate.shape[1]
        own_rows = layer_input.shape[0]
        group_rows = own_rows * tensor_size
        features = layer_input.shape[1]
        width = features // dp_size
        scale = HEAD_SIZE ** (-0.5)

        dp_index = lax.axis_index("dp")
        ring_index, pair_index = dp_index // PAIR, dp_index % PAIR
        tensor_index = lax.axis_index("tensor")
        order = [
            ((ring_index - j) % ring) * PAIR + (pair_index ^ e)
            for j in range(ring)
            for e in range(PAIR)
        ]
        back = [
            ((ring_index - b // PAIR) % ring) * PAIR + ((b % PAIR) ^ pair_index)
            for b in range(dp_size)
        ]

        def blocks(value, places):
            axis = value.ndim - 1
            return jnp.concatenate(
                [lax.dynamic_slice_in_dim(value, p * width, width, axis) for p in places], axis=axis
            )

        def row_block(value, p):
            return lax.slice_in_dim(value, p * own_rows, (p + 1) * own_rows, axis=0)

        def feature_block(value, i):
            return lax.slice_in_dim(value, i * width, (i + 1) * width, axis=1)

        attn_gain = blocks(attn_gain, order)
        mlp_gain = blocks(mlp_gain, order)
        inputs = wide(blocks(layer_input, order))
        out_grad = blocks(out_grad, order)

        inverse_first = inverse_rms(inputs)
        unit_first = inputs * inverse_first
        normed = low(unit_first * attn_gain)
        gathered = gather_rows(normed)

        attn_full = gather_weight(
            jnp.concatenate([w_query, key_projection, value_projection, w_out.T], axis=1), 0
        )
        joint_weight = attn_full[:, : width_q + 2 * width_kv]
        out_weight = attn_full[:, width_q + 2 * width_kv :]
        gate_up_weight = gather_weight(jnp.concatenate([w_gate, w_up], axis=1), 0)
        down_weight = gather_weight(w_down, 1)
        out_piece = gather_rows(out_grad)

        projected = dot("tc,ck->tk", gathered, joint_weight)
        query_raw = projected[:, :width_q].reshape(group_rows, head_q, HEAD_SIZE)
        key_raw = projected[:, width_q : width_q + width_kv].reshape(group_rows, head_kv, HEAD_SIZE)
        value_heads = low(projected[:, width_q + width_kv :]).reshape(
            group_rows, head_kv, HEAD_SIZE
        )
        inverse_query = inverse_rms(query_raw)
        unit_query = query_raw * inverse_query
        inverse_key = inverse_rms(key_raw)
        unit_key = key_raw * inverse_key
        half = HEAD_SIZE // 2
        true_rows = jnp.concatenate(
            [(tensor_index ^ p) * own_rows + jnp.arange(own_rows) for p in range(tensor_size)]
        )
        local_positions = jnp.concatenate(
            [
                lax.dynamic_slice_in_dim(positions, (tensor_index ^ p) * own_rows, own_rows, 0)
                for p in range(tensor_size)
            ]
        )
        frequency = jnp.power(THETA, -(2.0 * jnp.arange(half, dtype=jnp.float32)) / HEAD_SIZE)
        angle = local_positions.astype(jnp.float32)[:, None] * frequency[None, :]
        cosine_table = jnp.cos(angle)[:, None, :]
        sine_table = jnp.sin(angle)[:, None, :]
        query_heads = low(apply_rotary(unit_query * query_gain, cosine_table, sine_table))
        query_heads = query_heads.reshape(group_rows, head_kv, query_groups, HEAD_SIZE)
        key_heads = low(apply_rotary(unit_key * key_norm_gain, cosine_table, sine_table))
        visible = (true_rows[None, :] <= true_rows[:, None]) | (
            true_rows[None, :] < prefix_length[0]
        )

        block = 512
        spans = [(s, s + block) for s in range(0, group_rows, block)]

        def block_scores(begin, end):
            scores = dot("qkgd,skd->kgqs", query_heads[begin:end], key_heads) * scale
            return jnp.where(visible[begin:end], scores, -jnp.inf)

        mixed_blocks, log_totals = [], []
        for begin, end in spans:
            scores = block_scores(begin, end)
            largest = jnp.max(scores, axis=-1, keepdims=True)
            weights = jnp.exp(scores - largest)
            total = jnp.sum(weights, axis=-1, keepdims=True)
            probs = low(weights / total)
            mixed_blocks.append(low(dot("kgqs,skd->qkgd", probs, value_heads)))
            log_totals.append(largest + jnp.log(total))
        mixed = jnp.concatenate(mixed_blocks, axis=0).reshape(group_rows, width_q)

        branch = scatter_rows(lambda p: dot("th,ch->tc", row_block(mixed, p), out_weight))
        hidden = inputs + branch
        inverse_second = inverse_rms(hidden)
        unit_second = hidden * inverse_second
        normed_second = low(unit_second * mlp_gain)
        gathered_second = gather_rows(normed_second)

        gate_up = dot("tc,cf->tf", gathered_second, gate_up_weight)
        gate, upward = gate_up[:, :hidden_units], gate_up[:, hidden_units:]
        sigma = jax.nn.sigmoid(gate)
        activated = low(gate * sigma * upward)
        branch_second = scatter_rows(lambda p: dot("tf,fc->tc", row_block(activated, p), down_weight))
        layer_output = blocks(low(hidden + branch_second), back)

        down_grad = scatter_grad(
            lambda i: dot("tf,tc->fc", activated, feature_block(out_piece, i))
        )
        activated_grad = dot("tc,fc->tf", out_piece, down_weight)
        gate_grad = low(activated_grad * upward * sigma * (1.0 + gate * (1.0 - sigma)))
        up_grad = low(activated_grad * gate * sigma)
        gate_up_grad = jnp.concatenate([gate_grad, up_grad], axis=1)
        normed_second_grad = scatter_rows(
            lambda p: dot("tf,cf->tc", row_block(gate_up_grad, p), gate_up_weight)
        )
        gate_up_weight_grad = scatter_grad(
            lambda i: dot("tc,tf->cf", feature_block(gathered_second, i), gate_up_grad)
        )
        mlp_gain_part = jnp.sum(normed_second_grad * unit_second, axis=0)
        hidden_grad = wide(out_grad) + norm_back(
            normed_second_grad, unit_second, inverse_second, mlp_gain
        )
        branch_piece = gather_rows(low(hidden_grad))
        out_weight_grad = scatter_grad(
            lambda i: dot("th,tc->hc", mixed, feature_block(branch_piece, i))
        )
        mixed_grad = low(dot("tc,ch->th", branch_piece, out_weight)).reshape(
            group_rows, head_kv, query_groups, HEAD_SIZE
        )

        keys_grad = jnp.zeros((group_rows, head_kv, HEAD_SIZE), jnp.float32)
        values_grad = jnp.zeros((group_rows, head_kv, HEAD_SIZE), jnp.float32)
        query_blocks = []
        for (begin, end), log_total in zip(spans, log_totals):
            probs = jnp.exp(block_scores(begin, end) - log_total)
            grad_rows = mixed_grad[begin:end]
            probs_grad = dot("qkgd,skd->kgqs", grad_rows, value_heads)
            delta = jnp.sum(probs * probs_grad, axis=-1, keepdims=True)
            scores_grad = low(probs * (probs_grad - delta))
            query_blocks.append(dot("kgqs,skd->qkgd", scores_grad, key_heads) * scale)
            keys_grad += dot("kgqs,qkgd->skd", scores_grad, query_heads[begin:end]) * scale
            values_grad += dot("kgqs,qkgd->skd", low(probs), grad_rows)
        queries_grad = jnp.concatenate(query_blocks, axis=0).reshape(
            group_rows, head_q, HEAD_SIZE
        )
        query_norm_grad = apply_rotary(queries_grad, cosine_table, -sine_table)
        key_norm_grad = apply_rotary(keys_grad, cosine_table, -sine_table)
        query_gain_part = jnp.sum(query_norm_grad * unit_query, axis=(0, 1))
        key_gain_part = jnp.sum(key_norm_grad * unit_key, axis=(0, 1))
        query_raw_grad = low(norm_back(query_norm_grad, unit_query, inverse_query, query_gain))
        key_raw_grad = low(norm_back(key_norm_grad, unit_key, inverse_key, key_norm_gain))
        joint_grad = jnp.concatenate(
            [
                query_raw_grad.reshape(group_rows, width_q),
                key_raw_grad.reshape(group_rows, width_kv),
                low(values_grad).reshape(group_rows, width_kv),
            ],
            axis=1,
        )
        normed_grad = scatter_rows(
            lambda p: dot("tk,ck->tc", row_block(joint_grad, p), joint_weight)
        )
        joint_weight_grad = scatter_grad(
            lambda i: dot("tc,tk->ck", feature_block(gathered, i), joint_grad)
        )
        attn_gain_part = jnp.sum(normed_grad * unit_first, axis=0)
        input_grad = blocks(
            low(hidden_grad + norm_back(normed_grad, unit_first, inverse_first, attn_gain)), back
        )
        gains = lax.psum(
            (blocks(attn_gain_part, back), query_gain_part, key_gain_part, blocks(mlp_gain_part, back)),
            ("dp", "tensor"),
        )
        return (
            layer_output,
            input_grad,
            gains[0],
            joint_weight_grad[:, :width_q],
            joint_weight_grad[:, width_q : width_q + width_kv],
            joint_weight_grad[:, width_q + width_kv :],
            gains[1],
            gains[2],
            out_weight_grad,
            gains[3],
            gate_up_weight_grad[:, :hidden_units],
            gate_up_weight_grad[:, hidden_units:],
            down_grad,
        )

    return local


def solution(mesh):
    return jax.shard_map(
        build(mesh.shape["dp"], mesh.shape["tensor"]),
        mesh=mesh,
        in_specs=(
            P(("dp", "tensor"), None),
            P(("dp", "tensor"), None),
            P("dp"),
            P("dp"),
            P(),
            P("dp", "tensor"),
            P("dp", "tensor"),
            P("dp", "tensor"),
            P(),
            P(),
            P("tensor", "dp"),
            P(),
            P("dp", "tensor"),
            P("dp", "tensor"),
            P("tensor", "dp"),
        ),
        out_specs=(
            P(("dp", "tensor"), None),
            P(("dp", "tensor"), None),
            P(),
            P("dp", "tensor"),
            P("dp", "tensor"),
            P("dp", "tensor"),
            P(),
            P(),
            P("tensor", "dp"),
            P(),
            P("dp", "tensor"),
            P("dp", "tensor"),
            P("tensor", "dp"),
        ),
        check_vma=False,
    )
```

```python
import jax
import jax.numpy as jnp
from jax import lax
from jax.sharding import PartitionSpec as P


HEAD_SIZE = 128
EPS = 1e-06
THETA = 1000000.0
PAIR = 2


def inverse_rms(value_heads):
    return lax.rsqrt(jnp.mean(value_heads * value_heads, axis=-1, keepdims=True) + EPS)


def norm_back(grad, unit, inverse, gain):
    scaled = grad * gain
    return inverse * (scaled - unit * jnp.mean(scaled * unit, axis=-1, keepdims=True))


def apply_rotary(value_heads, cosine_table, sine_table):
    half = value_heads.shape[-1] // 2
    first = value_heads[..., :half]
    second = value_heads[..., half:]
    return jnp.concatenate(
        [first * cosine_table - second * sine_table, second * cosine_table + first * sine_table],
        axis=-1,
    )


def dot(equation, left, right):
    return jnp.einsum(equation, left, right, preferred_element_type=jnp.float32)


def low(value):
    return value.astype(jnp.bfloat16)


def wide(value):
    return value.astype(jnp.float32)


def build(dp_size, tensor_size):
    ring = dp_size // PAIR
    pair_perm = [(i, i ^ 1) for i in range(dp_size)]
    across_perm = [(i, i ^ 2) for i in range(tensor_size)]
    core_perm = [(i, i ^ 1) for i in range(tensor_size)]
    both_perm = [(i, i ^ 3) for i in range(tensor_size)]

    def ring_shift(value, hops=1):
        perm = [
            (a * PAIR + b, ((a + hops) % ring) * PAIR + b) for a in range(ring) for b in range(PAIR)
        ]
        return lax.ppermute(value, "dp", perm)

    def pair_swap(value):
        return lax.ppermute(value, "dp", pair_perm)

    def across_swap(value):
        return lax.ppermute(value, "tensor", across_perm)

    def core_swap(value):
        return lax.ppermute(value, "tensor", core_perm)

    def both_swap(value):
        return lax.ppermute(value, "tensor", both_perm)

    def gather_weight(shard, axis, halve):
        pieces = []
        held = shard
        for step in range(ring):
            if step:
                held = ring_shift(held)
            pieces.append(held)
            if halve and step == ring - 1:
                near, far = jnp.split(held, 2, axis=1 - axis)
                del far
                passed = jnp.split(pieces[-2], 2, axis=1 - axis)[1]
                pieces.append(
                    jnp.concatenate(
                        [pair_swap(near), ring_shift(passed)],
                        axis=1 - axis,
                    )
                )
            else:
                pieces.append(pair_swap(held))
        return pieces

    def scatter_grad(chunk):
        total = None
        for step in range(1, ring + 1):
            place = step % ring
            other = chunk(PAIR * place + 1)
            if step == 1:
                near, far = jnp.split(other, 2, axis=0)
                passed = ring_shift(low(far))
                rows = near.shape[0]
                arrived = pair_swap(low(near))
                own = chunk(PAIR * place)
                total = jnp.concatenate([own[:rows] + wide(arrived), own[rows:]], axis=0)
                continue
            if step == 2:
                other = jnp.concatenate([other[:rows], other[rows:] + wide(passed)], axis=0)
            arrived = pair_swap(low(other))
            part = chunk(PAIR * place) + wide(arrived)
            total = part + wide(ring_shift(low(total)))
        return total

    def sum_everywhere(value):
        value = value + core_swap(value) + across_swap(value) + both_swap(value)
        value = value + pair_swap(value)
        return value + sum(ring_shift(value, hops) for hops in range(1, ring))

    def gather_rows(rows):
        far = across_swap(rows)
        return jnp.concatenate([rows, core_swap(rows), far, core_swap(far)], axis=0)

    def scatter_rows(parts):
        near = core_swap(low(parts(3)))
        send = low(parts(2) + wide(near))
        far = across_swap(send)
        close = core_swap(low(parts(1)))
        return parts(0) + wide(close) + wide(far)

    def local(
        layer_input,
        out_grad,
        prefix_length,
        positions,
        attn_gain,
        w_query,
        key_projection,
        value_projection,
        query_gain,
        key_norm_gain,
        w_out,
        mlp_gain,
        w_gate,
        w_up,
        w_down,
    ):
        head_q = w_query.shape[1] // HEAD_SIZE
        head_kv = key_projection.shape[1] // HEAD_SIZE
        query_groups = head_q // head_kv
        width_q = head_q * HEAD_SIZE
        width_kv = head_kv * HEAD_SIZE
        hidden_units = w_gate.shape[1]
        own_rows = layer_input.shape[0]
        group_rows = own_rows * tensor_size
        features = layer_input.shape[1]
        width = features // dp_size
        scale = HEAD_SIZE ** (-0.5)

        dp_index = lax.axis_index("dp")
        ring_index, pair_index = dp_index // PAIR, dp_index % PAIR
        tensor_index = lax.axis_index("tensor")
        order = [
            ((ring_index - j) % ring) * PAIR + (pair_index ^ e)
            for j in range(ring)
            for e in range(PAIR)
        ]
        back = [
            ((ring_index - b // PAIR) % ring) * PAIR + ((b % PAIR) ^ pair_index)
            for b in range(dp_size)
        ]

        def blocks(value, places):
            axis = value.ndim - 1
            return jnp.concatenate(
                [lax.dynamic_slice_in_dim(value, p * width, width, axis) for p in places], axis=axis
            )

        def row_block(value, p):
            return lax.slice_in_dim(value, p * own_rows, (p + 1) * own_rows, axis=0)

        def feature_block(value, i):
            return lax.slice_in_dim(value, i * width, (i + 1) * width, axis=1)

        attn_gain = blocks(attn_gain, order)
        mlp_gain = blocks(mlp_gain, order)
        inputs = wide(blocks(layer_input, order))
        out_grad = blocks(out_grad, order)

        inverse_first = inverse_rms(inputs)
        unit_first = inputs * inverse_first
        normed = low(unit_first * attn_gain)
        gathered = gather_rows(normed)

        half_width = width // 2
        joint_weight = jnp.concatenate(
            gather_weight(
                jnp.concatenate([w_query, key_projection, value_projection], axis=1), 0, False
            ),
            axis=0,
        )
        out_weight = jnp.concatenate(gather_weight(w_out, 1, False), axis=1)
        gate_up = jnp.concatenate([w_gate, w_up], axis=1)
        pieces_a = gather_weight(gate_up[:half_width], 0, True)
        pieces_b = gather_weight(gate_up[half_width:], 0, True)
        gate_up_weight = jnp.concatenate(
            [piece for pair in zip(pieces_a, pieces_b) for piece in pair], axis=0
        )
        pieces_a = gather_weight(w_down[:, :half_width], 1, True)
        pieces_b = gather_weight(w_down[:, half_width:], 1, True)
        down_weight = jnp.concatenate(
            [piece for pair in zip(pieces_a, pieces_b) for piece in pair], axis=1
        )
        out_piece = gather_rows(out_grad)

        projected = dot("tc,ck->tk", gathered, joint_weight)
        query_raw = projected[:, :width_q].reshape(group_rows, head_q, HEAD_SIZE)
        key_raw = projected[:, width_q : width_q + width_kv].reshape(group_rows, head_kv, HEAD_SIZE)
        value_heads = low(projected[:, width_q + width_kv :]).reshape(
            group_rows, head_kv, HEAD_SIZE
        )
        inverse_query = inverse_rms(query_raw)
        unit_query = query_raw * inverse_query
        inverse_key = inverse_rms(key_raw)
        unit_key = key_raw * inverse_key
        half = HEAD_SIZE // 2
        true_rows = jnp.concatenate(
            [(tensor_index ^ p) * own_rows + jnp.arange(own_rows) for p in range(tensor_size)]
        )
        local_positions = jnp.concatenate(
            [
                lax.dynamic_slice_in_dim(positions, (tensor_index ^ p) * own_rows, own_rows, 0)
                for p in range(tensor_size)
            ]
        )
        frequency = jnp.power(THETA, -(2.0 * jnp.arange(half, dtype=jnp.float32)) / HEAD_SIZE)
        angle = local_positions.astype(jnp.float32)[:, None] * frequency[None, :]
        cosine_table = jnp.cos(angle)[:, None, :]
        sine_table = jnp.sin(angle)[:, None, :]
        query_heads = low(apply_rotary(unit_query * query_gain, cosine_table, sine_table))
        query_heads = query_heads.reshape(group_rows, head_kv, query_groups, HEAD_SIZE)
        key_heads = low(apply_rotary(unit_key * key_norm_gain, cosine_table, sine_table))
        visible = (true_rows[None, :] <= true_rows[:, None]) | (
            true_rows[None, :] < prefix_length[0]
        )

        block = 512
        spans = [(s, s + block) for s in range(0, group_rows, block)]

        def block_scores(begin, end):
            scores = dot("qkgd,skd->kgqs", query_heads[begin:end], key_heads) * scale
            return jnp.where(visible[begin:end], scores, -jnp.inf)

        mixed_blocks, log_totals = [], []
        for begin, end in spans:
            scores = block_scores(begin, end)
            largest = jnp.max(scores, axis=-1, keepdims=True)
            weights = jnp.exp(scores - largest)
            total = jnp.sum(weights, axis=-1, keepdims=True)
            probs = low(weights / total)
            mixed_blocks.append(low(dot("kgqs,skd->qkgd", probs, value_heads)))
            log_totals.append(largest + jnp.log(total))
        mixed = jnp.concatenate(mixed_blocks, axis=0).reshape(group_rows, width_q)

        branch = scatter_rows(lambda p: dot("th,hc->tc", row_block(mixed, p), out_weight))
        hidden = inputs + branch
        inverse_second = inverse_rms(hidden)
        unit_second = hidden * inverse_second
        normed_second = low(unit_second * mlp_gain)
        gathered_second = gather_rows(normed_second)

        gate_up = dot("tc,cf->tf", gathered_second, gate_up_weight)
        gate, upward = gate_up[:, :hidden_units], gate_up[:, hidden_units:]
        sigma = jax.nn.sigmoid(gate)
        activated = low(gate * sigma * upward)
        branch_second = scatter_rows(lambda p: dot("tf,fc->tc", row_block(activated, p), down_weight))
        layer_output = blocks(low(hidden + branch_second), back)

        down_grad = scatter_grad(lambda i: dot("tf,tc->fc", activated, feature_block(out_piece, i)))
        activated_grad = dot("tc,fc->tf", out_piece, down_weight)
        gate_grad = low(activated_grad * upward * sigma * (1.0 + gate * (1.0 - sigma)))
        up_grad = low(activated_grad * gate * sigma)
        gate_up_grad = jnp.concatenate([gate_grad, up_grad], axis=1)
        normed_second_grad = scatter_rows(
            lambda p: dot("tf,cf->tc", row_block(gate_up_grad, p), gate_up_weight)
        )
        gate_weight_grad = scatter_grad(
            lambda i: dot("tc,tf->cf", feature_block(gathered_second, i), gate_grad)
        )
        up_weight_grad = scatter_grad(
            lambda i: dot("tc,tf->cf", feature_block(gathered_second, i), up_grad)
        )
        mlp_gain_part = jnp.sum(normed_second_grad * unit_second, axis=0)
        hidden_grad = wide(out_grad) + norm_back(
            normed_second_grad, unit_second, inverse_second, mlp_gain
        )
        branch_piece = gather_rows(low(hidden_grad))
        out_weight_grad = scatter_grad(
            lambda i: dot("th,tc->hc", mixed, feature_block(branch_piece, i))
        )
        mixed_grad = low(dot("tc,hc->th", branch_piece, out_weight)).reshape(
            group_rows, head_kv, query_groups, HEAD_SIZE
        )

        keys_grad = jnp.zeros((group_rows, head_kv, HEAD_SIZE), jnp.float32)
        values_grad = jnp.zeros((group_rows, head_kv, HEAD_SIZE), jnp.float32)
        query_blocks = []
        for (begin, end), log_total in zip(spans, log_totals):
            probs = jnp.exp(block_scores(begin, end) - log_total)
            grad_rows = mixed_grad[begin:end]
            probs_grad = dot("qkgd,skd->kgqs", grad_rows, value_heads)
            delta = jnp.sum(probs * probs_grad, axis=-1, keepdims=True)
            scores_grad = low(probs * (probs_grad - delta))
            query_blocks.append(dot("kgqs,skd->qkgd", scores_grad, key_heads) * scale)
            keys_grad += dot("kgqs,qkgd->skd", scores_grad, query_heads[begin:end]) * scale
            values_grad += dot("kgqs,qkgd->skd", low(probs), grad_rows)
        queries_grad = jnp.concatenate(query_blocks, axis=0).reshape(
            group_rows, head_q, HEAD_SIZE
        )
        query_norm_grad = apply_rotary(queries_grad, cosine_table, -sine_table)
        key_norm_grad = apply_rotary(keys_grad, cosine_table, -sine_table)
        query_gain_part = jnp.sum(query_norm_grad * unit_query, axis=(0, 1))
        key_gain_part = jnp.sum(key_norm_grad * unit_key, axis=(0, 1))
        query_raw_grad = low(norm_back(query_norm_grad, unit_query, inverse_query, query_gain))
        key_raw_grad = low(norm_back(key_norm_grad, unit_key, inverse_key, key_norm_gain))
        joint_grad = jnp.concatenate(
            [
                query_raw_grad.reshape(group_rows, width_q),
                key_raw_grad.reshape(group_rows, width_kv),
                low(values_grad).reshape(group_rows, width_kv),
            ],
            axis=1,
        )
        normed_grad = scatter_rows(
            lambda p: dot("tk,ck->tc", row_block(joint_grad, p), joint_weight)
        )
        query_weight_grad = scatter_grad(
            lambda i: dot("tc,tk->ck", feature_block(gathered, i), joint_grad[:, :width_q])
        )
        pair_weight_grad = scatter_grad(
            lambda i: dot("tc,tk->ck", feature_block(gathered, i), joint_grad[:, width_q:])
        )
        attn_gain_part = jnp.sum(normed_grad * unit_first, axis=0)
        input_grad = blocks(
            low(hidden_grad + norm_back(normed_grad, unit_first, inverse_first, attn_gain)), back
        )
        early = sum_everywhere(
            jnp.concatenate([blocks(mlp_gain_part, back), query_gain_part, key_gain_part]).reshape(
                -1, HEAD_SIZE
            )
        ).reshape(-1)
        late = sum_everywhere(blocks(attn_gain_part, back).reshape(-1, HEAD_SIZE)).reshape(-1)
        return (
            layer_output,
            input_grad,
            late,
            query_weight_grad,
            pair_weight_grad[:, :width_kv],
            pair_weight_grad[:, width_kv:],
            early[features : features + HEAD_SIZE],
            early[features + HEAD_SIZE :],
            out_weight_grad,
            early[:features],
            gate_weight_grad,
            up_weight_grad,
            down_grad,
        )

    return local


def solution(mesh):
    body = build(mesh.shape["dp"], mesh.shape["tensor"])

    return jax.shard_map(
        body,
        mesh=mesh,
        in_specs=(
            P(("dp", "tensor"), None),
            P(("dp", "tensor"), None),
            P("dp"),
            P("dp"),
            P(),
            P("dp", "tensor"),
            P("dp", "tensor"),
            P("dp", "tensor"),
            P(),
            P(),
            P("tensor", "dp"),
            P(),
            P("dp", "tensor"),
            P("dp", "tensor"),
            P("tensor", "dp"),
        ),
        out_specs=(
            P(("dp", "tensor"), None),
            P(("dp", "tensor"), None),
            P(),
            P("dp", "tensor"),
            P("dp", "tensor"),
            P("dp", "tensor"),
            P(),
            P(),
            P("tensor", "dp"),
            P(),
            P("dp", "tensor"),
            P("dp", "tensor"),
            P("tensor", "dp"),
        ),
        check_vma=False,
    )
```
